256 devices in a mesh: wide: 32 (over z, y_lo, core), narrow: 8 (over y_hi, x).
Axes of the slice: x: 4, y: 4 (y_hi: 2, y_lo: 2; y = y_hi * 2 + y_lo), z: 8, core: 2. Of those that a mesh axis runs over, the one named last changes fastest.
Arguments:
- vol_points: float32 [3, 65536], P(None, 'wide'), may hold values from 0 to 1
- vol_adjoint: bfloat16 [48, 65536], P(None, 'wide'), may hold values from -6 to 6
- surf_points: float32 [3, 32768], P(None, ('narrow', 'wide')), may hold values from 0 to 1
- tile_mask: int32 [512, 256], P('wide', 'narrow'), may hold values 0 or 1
Outputs:
- solution: float32 [48, 32768], P(None, ('narrow', 'wide'))
- residual: float32 [48, 32768], P(None, ('narrow', 'wide'))
The draws below stay inside these ranges and needn't reach their ends.
All inputs are finite; a program needn't handle non-finite values. No bound on the sum of `tile_mask` on one device may be relied on, other than what follows from the above.
Results may differ from the reference program's by a relative error of at most 0.0039.
Values sent between devices are 32-bit elements; how exact they have to be, the bound alone decides.
No kernel may reach another device: no remote copies, remote signals or barrier semaphores. Data moves between devices by JAX's collectives and lax.ppermute only.
A program may use at most 64 MiB of HBM per device.

```python
import math
import jax
import jax.numpy as jnp
from jax import lax

OBJ_COLS = 48
TILE = 128
NV = 65536
NS = 32768


def place_ends(drawn, rng, smallest, largest):
    longest = drawn.shape.index(max(drawn.shape))
    spots = []
    for shift in (0, 1):
        where = [jax.random.randint(jax.random.fold_in(rng, axis), (), 0, length) for axis, length in enumerate(drawn.shape)]
        where[longest] = (where[longest] + shift) % drawn.shape[longest]
        spots.append(tuple(where))
    return drawn.at[spots[0]].set(smallest).at[spots[1]].set(largest)


def block_scale(own_key, dims, shards, low, largest):
    def one(dim, shards_of):
        steps = jax.random.uniform(jax.random.fold_in(jax.random.fold_in(own_key, 6), dim), (shards_of,), jnp.float32, low / len(shards), largest / len(shards))
        return jnp.repeat(jnp.exp(steps), dims[dim] // shards_of).reshape((-1,) + (1,) * (len(dims) - dim - 1))

    gain = one(*shards[0])
    for cut in shards[1:]:
        gain = gain * one(*cut)
    return gain


def scatter_about(key, shape, spread, limit, split=(), dtype=jnp.bfloat16):
    entries = jax.random.normal(key, shape, jnp.float32) * spread
    if len(split) > 0:
        entries = block_scale(key, shape, split, -0.22, 0.18) * entries
    return jnp.clip(entries, min=-limit, max=limit).astype(dtype)


def setup_inputs(seed: int = 0) -> dict:
    splits = jax.random.split(jax.random.key(seed), 5)
    return {
        "vol_points": jnp.clip(1.0 * jax.random.uniform(splits[0], (3, NV), jnp.float32) ** block_scale(splits[0], (3, NV), ((1, 32),), -0.2, 0.2), 0.0, 1.0),
        "vol_adjoint": scatter_about(splits[1], (OBJ_COLS, NV), 1.0, 6.0, ((1, 32),)),
        "surf_points": jnp.clip(1.0 * jax.random.uniform(splits[2], (3, NS), jnp.float32) ** block_scale(splits[2], (3, NS), ((1, 256),), -0.2, 0.2), 0.0, 1.0),
        "tile_mask": place_ends((jax.random.randint(splits[3], (NV // TILE, NS // TILE), 0, 4) < 3).astype(jnp.int32), jax.random.fold_in(splits[3], 1), 0, 1),
    }


RADIUS = 0.15
KERNEL_GAIN = 3200.0
RHS_GAIN = 28.0
LOWER_EDGE = 1.0
UPPER_EDGE = 4.0

def kernel_block(sources, targets):
    squared = jnp.zeros((sources.shape[1], targets.shape[1]), jnp.float32)
    for component in range(3):
        offset = sources[component][:, None] - targets[component][None, :]
        squared = squared + offset * offset
    scaled = jnp.sqrt(squared) / RADIUS
    remain = jnp.maximum(1.0 - scaled, 0.0)
    return remain ** 4 * (4.0 * scaled + 1.0)

def apply_operator(field, surf_points):
    width = math.gcd(NS, 512)

    def row_block(index):
        start = (index * width).astype(jnp.int32)
        targets = lax.dynamic_slice_in_dim(surf_points, start, width, 1)
        values = kernel_block(surf_points, targets)
        return jnp.dot(field, values, precision=lax.Precision.HIGHEST, preferred_element_type=jnp.float32)
    blocks = lax.map(row_block, jnp.arange(NS // width).astype(jnp.int32))
    mixed = jnp.transpose(blocks, (1, 0, 2)).reshape(field.shape[0], NS)
    return field + KERNEL_GAIN / NS * mixed

def reference(vol_points, vol_adjoint, surf_points, tile_mask):
    width = math.gcd(NS, 512)

    def column_block(index):
        start = (index * width).astype(jnp.int32)
        targets = lax.dynamic_slice_in_dim(surf_points, start, width, 1)
        mask_cols = lax.dynamic_slice_in_dim(tile_mask, (start // TILE).astype(jnp.int32), width // TILE, 1)
        expanded = jnp.repeat(jnp.repeat(mask_cols, TILE, 0), TILE, 1).astype(jnp.float32)
        values = (kernel_block(vol_points, targets) * expanded).astype(jnp.bfloat16)
        return jnp.dot(vol_adjoint, values, preferred_element_type=jnp.float32)
    blocks = lax.map(column_block, jnp.arange(NS // width).astype(jnp.int32))
    summed = jnp.transpose(blocks, (1, 0, 2)).reshape(vol_adjoint.shape[0], NS)
    rhs = summed * (RHS_GAIN / math.sqrt(NV))
    centre = (LOWER_EDGE + UPPER_EDGE) / 2.0
    half_width = (UPPER_EDGE - LOWER_EDGE) / 2.0
    sigma = centre / half_width
    rho_zero = 1.0 / sigma
    rho_one = 1.0 / (2.0 * sigma - rho_zero)
    first = rhs / centre
    near = rhs - apply_operator(first, surf_points)
    update = rho_one * rho_zero * first + 2.0 * rho_one / half_width * near
    solution = first + update
    residual = near - apply_operator(update, surf_points)
    return (solution, residual)
```

```python
import functools
import math

import jax
import jax.numpy as jnp
from jax import lax
from jax.experimental import pallas as pl
from jax.experimental.pallas import tpu as pltpu
from jax.sharding import PartitionSpec as P

TILE = 128
RADIUS = 0.15
KERNEL_GAIN = 3200.0
RHS_GAIN = 28.0
LOWER_EDGE = 1.0
UPPER_EDGE = 4.0

SCALE = 4.0 / RADIUS
PHI = 1.0 / 256.0
FAR = 4096.0
DEPTH = 128


def split3(x):
    one = x.astype(jnp.bfloat16).astype(jnp.float32)
    rest = x - one
    two = rest.astype(jnp.bfloat16).astype(jnp.float32)
    return one, two, rest - two


def features(points, target, extra=None):
    count = points.shape[1]
    centred = (points - 0.5) * SCALE
    norm = jnp.sum(centred * centred, axis=0, keepdims=True)
    n1, n2, n3 = split3(jnp.broadcast_to(norm, (8, count)))
    row = lax.broadcasted_iota(jnp.int32, (8, count), 0)
    one, zero = jnp.ones_like(n1), jnp.zeros_like(n1)
    if target:
        c1, c2, c3 = split3(-2.0 * centred)
        tail = jnp.where(row < 3, one, jnp.where(row == 3, n1, jnp.where(row == 4, n2, jnp.where(row == 5, n3, zero))))
        groups = [c1, c2, c1, c2, c3, c1, tail]
    else:
        c1, c2, c3 = split3(centred)
        tail = jnp.where(row == 0, n1, jnp.where(row == 1, n2, jnp.where(row == 2, n3, jnp.where(row < 6, one, zero))))
        groups = [c1, c1, c2, c2, c1, c3, tail]
    used = 8 * len(groups)
    if extra is not None:
        groups.append(extra)
        used += extra.shape[0]
    groups.append(jnp.zeros((DEPTH - used, count), jnp.float32))
    return jnp.concatenate(groups, axis=0)


def profile(d2):
    d2 = jnp.maximum(d2, 1e-12)
    w = jnp.maximum(4.0 - d2 * lax.rsqrt(d2), 0.0)
    square = w * w
    return (square * square) * (5.0 - w)


def coupling_kernel(spot_ref, vol_ref, adj_ref, mask_ref, cols_ref, keep_ref, send_ref, feat_ref):
    rows = vol_ref.shape[1]
    tiles = rows // TILE
    width = cols_ref.shape[2]

    @pl.when(pl.program_id(0) == 0)
    def _():
        tile = lax.broadcasted_iota(jnp.int32, (tiles, rows), 0)
        place = lax.broadcasted_iota(jnp.int32, (tiles, rows), 1) // TILE
        onehot = jnp.where(tile == place, 1.0, 0.0)
        feat_ref[...] = features(vol_ref[...], False, onehot).T.astype(jnp.bfloat16)

    cols_tiles = mask_ref.shape[1]
    tile = lax.broadcasted_iota(jnp.int32, (cols_tiles, width), 0)
    piece = lax.broadcasted_iota(jnp.int32, (cols_tiles, width), 1) // TILE
    swapped = (piece % 2) * 2 + piece // 2
    owner = 4 * pl.program_id(0) + (swapped ^ spot_ref[0])
    pick = jnp.where(tile == owner, 1.0, 0.0).astype(jnp.bfloat16)
    absent = (1 - mask_ref[...]).astype(jnp.float32).astype(jnp.bfloat16)
    barred = FAR * jnp.dot(absent, pick, preferred_element_type=jnp.float32)
    target = features(cols_ref[0], True, barred).astype(jnp.bfloat16)

    total = jnp.zeros((adj_ref.shape[0], width), jnp.float32)
    step = 256
    for start in range(0, rows, step):
        d2 = jnp.dot(feat_ref[start:start + step, :], target, preferred_element_type=jnp.float32)
        values = profile(d2).astype(jnp.bfloat16)
        total += jnp.dot(adj_ref[:, start:start + step], values, preferred_element_type=jnp.float32)
    half = width // 2
    keep_ref[0] = total[:, :half]
    send_ref[0] = total[:, half:]


def coupling(spot, vol, adj, mask, cols):
    blocks, _, width = cols.shape
    objs = adj.shape[0]
    whole = lambda shape: pl.BlockSpec(shape, lambda z, s: (0,) * len(shape))
    out = jax.ShapeDtypeStruct((blocks, objs, width // 2), jnp.float32)
    return pl.pallas_call(
        coupling_kernel,
        grid_spec=pltpu.PrefetchScalarGridSpec(
            num_scalar_prefetch=1,
            grid=(blocks,),
            in_specs=[
                whole(vol.shape),
                whole(adj.shape),
                whole(mask.shape),
                pl.BlockSpec((1, 8, width), lambda z, s: (z, 0, 0)),
            ],
            out_specs=[pl.BlockSpec((1, objs, width // 2), lambda z, s: (z, 0, 0))] * 2,
            scratch_shapes=[pltpu.VMEM((vol.shape[1], DEPTH), jnp.bfloat16)],
        ),
        out_shape=(out, out),
        name="coupling",
        cost_estimate=pl.CostEstimate(flops=20 * vol.shape[1] * blocks * width, bytes_accessed=2 << 20, transcendentals=0),
    )(spot, vol, adj, mask, cols)


def gram_kernel(cols_ref, rows_ref, out_ref, feat_ref):
    @pl.when(pl.program_id(0) == 0)
    def _():
        for j in range(rows_ref.shape[0]):
            feat_ref[:, j * TILE:(j + 1) * TILE] = features(rows_ref[j], True).astype(jnp.bfloat16)

    source = features(cols_ref[0], False).T.astype(jnp.bfloat16)
    width = out_ref.shape[2]
    step = 256
    for start in range(0, width, step):
        d2 = jnp.dot(source, feat_ref[:, start:start + step], preferred_element_type=jnp.float32)
        out_ref[0, :, start:start + step] = profile(d2).astype(jnp.bfloat16)


def gram(cols, rows):
    blocks, _, depth = cols.shape
    width = rows.shape[0] * rows.shape[2]
    return pl.pallas_call(
        gram_kernel,
        grid=(blocks,),
        in_specs=[
            pl.BlockSpec((1, 8, depth), lambda z: (z, 0, 0)),
            pl.BlockSpec(rows.shape, lambda z: (0, 0, 0)),
        ],
        out_specs=pl.BlockSpec((1, depth, width), lambda z: (z, 0, 0)),
        out_shape=jax.ShapeDtypeStruct((blocks, depth, width), jnp.bfloat16),
        scratch_shapes=[pltpu.VMEM((DEPTH, width), jnp.bfloat16)],
        name="gram",
        cost_estimate=pl.CostEstimate(flops=20 * blocks * depth * width, bytes_accessed=8 << 20, transcendentals=0),
    )(cols, rows)


def mix_kernel(keep_ref, send_ref, gram_ref, out_ref):
    blocks, objs, half = keep_ref.shape
    width = gram_ref.shape[2]
    total = jnp.zeros((2 * objs, width), jnp.float32)
    for z in range(blocks):
        for side, ref in enumerate((keep_ref, send_ref)):
            field = ref[z]
            high = field.astype(jnp.bfloat16).astype(jnp.float32)
            both = jnp.concatenate([high, field - high], axis=0).astype(jnp.bfloat16)
            values = gram_ref[z, side * half:(side + 1) * half, :]
            total += jnp.dot(both, values, preferred_element_type=jnp.float32)
    for j in range(out_ref.shape[0]):
        out_ref[j] = total[:objs, j * TILE:(j + 1) * TILE] + total[objs:, j * TILE:(j + 1) * TILE]


def mix(keep, send, block):
    blocks, objs, half = keep.shape
    _, depth, width = block.shape
    parts = width // TILE
    return pl.pallas_call(
        mix_kernel,
        in_specs=[pl.BlockSpec(memory_space=pltpu.VMEM)] * 3,
        out_specs=pl.BlockSpec(memory_space=pltpu.VMEM),
        out_shape=jax.ShapeDtypeStruct((parts, objs, TILE), jnp.float32),
        name="mix",
        cost_estimate=pl.CostEstimate(flops=4 * objs * blocks * depth * width, bytes_accessed=10 << 20, transcendentals=0),
    )(keep, send, block)


def body(n_wide, n_narrow, vol_points, vol_adjoint, surf_points, tile_mask):
    far = n_wide // 4
    groups = [[4 * z + r for z in range(far)] for r in range(4)]
    flip = lambda x, bit: lax.ppermute(x, "wide", [(i, i ^ bit) for i in range(n_wide)])
    exchange = lambda x: lax.all_to_all(x, "wide", 0, 0, axis_index_groups=groups, tiled=True)

    def spread(x):
        pair = jnp.concatenate([x, flip(x, 2)], axis=1)
        mine = exchange(jnp.broadcast_to(pair[None], (far,) + pair.shape))
        return mine, flip(mine, 1)

    pad = lambda p: jnp.pad(p, ((0, 5), (0, 0)), constant_values=0.5)
    own = pad(surf_points)
    near_cols, other_cols = spread(own)
    cols = jnp.concatenate([near_cols, other_cols], axis=2)
    rows = own[None]
    for bit in (4, 2, 1):
        rows = jnp.concatenate([rows, lax.ppermute(rows, "narrow", [(i, i ^ bit) for i in range(n_narrow)])], axis=0)
    order = [0]
    for bit in (4, 2, 1):
        order = order + [o ^ bit for o in order]
    spot = (lax.axis_index("wide") % 4).astype(jnp.int32).reshape(1)
    where = lax.axis_index("narrow")
    rows = jnp.stack([rows[order.index(j)] for j in range(n_narrow)], axis=0)
    wanted = jnp.arange(n_narrow, dtype=jnp.int32) ^ where
    rows = sort_rows(rows, wanted)

    keep, send = coupling(spot, pad(vol_points), vol_adjoint, tile_mask, cols)
    got = flip(send, 1)
    block = gram(cols, rows)
    summed = jnp.sum(exchange(keep + got), axis=0)
    both = summed + jnp.concatenate([x for x in halves(flip(summed, 2))], axis=1)
    total_volume = vol_points.shape[1] * n_wide
    total_surface = surf_points.shape[1] * n_wide * n_narrow
    centre = (LOWER_EDGE + UPPER_EDGE) / 2.0
    half_width = (UPPER_EDGE - LOWER_EDGE) / 2.0
    sigma = centre / half_width
    rho_zero = 1.0 / sigma
    rho_one = 1.0 / (2.0 * sigma - rho_zero)
    gain = KERNEL_GAIN / total_surface * PHI

    pair_rhs = both * (RHS_GAIN / math.sqrt(total_volume) * PHI)
    pair_first = pair_rhs / centre
    mine = exchange(jnp.broadcast_to(pair_first[None], (far,) + pair_first.shape))
    mixed = mix(mine, flip(mine, 1), block)
    collect = lambda m: jnp.sum(lax.all_to_all(m, "narrow", 0, 0, tiled=True), axis=0)
    rhs, first = pair_rhs[:, :TILE], pair_first[:, :TILE]
    near = rhs - (first + gain * collect(mixed))
    update = rho_one * rho_zero * first + 2.0 * rho_one / half_width * near
    solution = first + update
    mixed = mix(*spread(update), block)
    residual = near - (update + gain * collect(mixed))
    return (solution, residual)


def halves(x):
    return x[:, TILE:], x[:, :TILE]


def sort_kernel(wanted_ref, in_ref, out_ref):
    out_ref[...] = in_ref[...]


def sort_rows(rows, wanted):
    return pl.pallas_call(
        sort_kernel,
        grid_spec=pltpu.PrefetchScalarGridSpec(
            num_scalar_prefetch=1,
            grid=(rows.shape[0],),
            in_specs=[pl.BlockSpec((1,) + rows.shape[1:], lambda j, w: (w[j], 0, 0))],
            out_specs=pl.BlockSpec((1,) + rows.shape[1:], lambda j, w: (j, 0, 0)),
        ),
        out_shape=jax.ShapeDtypeStruct(rows.shape, rows.dtype),
        name="sort_rows",
    )(wanted, rows)


def solution(mesh):
    return jax.shard_map(
        functools.partial(body, mesh.shape["wide"], mesh.shape["narrow"]),
        mesh=mesh,
        in_specs=(
            P(None, "wide"),
            P(None, "wide"),
            P(None, ("narrow", "wide")),
            P("wide", "narrow"),
        ),
        out_specs=(P(None, ("narrow", "wide")), P(None, ("narrow", "wide"))),
        check_vma=False,
    )
```

```python
import functools
import math

import jax
import jax.numpy as jnp
from jax import lax
from jax.experimental import pallas as pl
from jax.experimental.pallas import tpu as pltpu
from jax.sharding import PartitionSpec as P


TILE = 128
RADIUS = 0.15
KERNEL_GAIN = 3200.0
RHS_GAIN = 28.0
LOWER_EDGE = 1.0
UPPER_EDGE = 4.0

SCALE = 4.0 / RADIUS
PHI = 1.0 / 256.0
FAR = 4096.0
DEPTH = 128
GRANT = 20 << 20


def split3(x):
    one = x.astype(jnp.bfloat16).astype(jnp.float32)
    rest = x - one
    two = rest.astype(jnp.bfloat16).astype(jnp.float32)
    return one, two, rest - two


def padded(points):
    fill = jnp.full((8 - points.shape[0], points.shape[1]), 0.5, jnp.float32)
    return jnp.concatenate([points, fill], axis=0)


def features(points, target, extra=None):
    count = points.shape[1]
    centred = (points - 0.5) * SCALE
    norm = jnp.sum(centred * centred, axis=0, keepdims=True)
    n1, n2, n3 = split3(jnp.broadcast_to(norm, (8, count)))
    row = lax.broadcasted_iota(jnp.int32, (8, count), 0)
    one, zero = jnp.ones_like(n1), jnp.zeros_like(n1)
    if target:
        c1, c2, c3 = split3(-2.0 * centred)
        tail = jnp.where(row < 3, one, jnp.where(row == 3, n1, jnp.where(row == 4, n2, jnp.where(row == 5, n3, zero))))
        groups = [c1, c2, c1, c2, c3, c1, tail]
    else:
        c1, c2, c3 = split3(centred)
        tail = jnp.where(row == 0, n1, jnp.where(row == 1, n2, jnp.where(row == 2, n3, jnp.where(row < 6, one, zero))))
        groups = [c1, c1, c2, c2, c1, c3, tail]
    used = 8 * len(groups)
    if extra is not None:
        groups.append(extra)
        used += extra.shape[0]
    groups.append(jnp.zeros((DEPTH - used, count), jnp.float32))
    return jnp.concatenate(groups, axis=0)


def profile(d2):
    d2 = jnp.maximum(d2, 1e-12)
    w = jnp.maximum(4.0 - d2 * lax.rsqrt(d2), 0.0)
    square = w * w
    return (square * square) * (5.0 - w)


def stage_kernel(vol_ref, adj_ref, mask_ref, feat_ref, weights_ref, absent_ref, near_ref, held_ref, sem_ref):
    copies = [
        pltpu.make_async_copy(vol_ref, near_ref, sem_ref.at[0]),
        pltpu.make_async_copy(mask_ref, held_ref, sem_ref.at[1]),
        pltpu.make_async_copy(adj_ref, weights_ref, sem_ref.at[2]),
    ]
    for copy in copies:
        copy.start()
    for copy in copies:
        copy.wait()
    rows = vol_ref.shape[1]
    tiles = rows // TILE
    tile = lax.broadcasted_iota(jnp.int32, (tiles, rows), 0)
    place = lax.broadcasted_iota(jnp.int32, (tiles, rows), 1) // TILE
    onehot = jnp.where(tile == place, 1.0, 0.0)
    feat_ref[...] = features(padded(near_ref[...]), False, onehot).T.astype(jnp.bfloat16)
    absent_ref[...] = (1 - held_ref[...]).astype(jnp.float32)


def stage(vol, adj, mask):
    return pl.pallas_call(
        stage_kernel,
        in_specs=[pl.BlockSpec(memory_space=pltpu.HBM)] * 3,
        out_specs=[pl.BlockSpec(memory_space=pltpu.VMEM)] * 3,
        out_shape=(
            jax.ShapeDtypeStruct((vol.shape[1], DEPTH), jnp.bfloat16),
            jax.ShapeDtypeStruct(adj.shape, jnp.bfloat16),
            jax.ShapeDtypeStruct(mask.shape, jnp.float32),
        ),
        scratch_shapes=[
            pltpu.VMEM(vol.shape, jnp.float32),
            pltpu.VMEM(mask.shape, jnp.int32),
            pltpu.SemaphoreType.DMA((3,)),
        ],
        name="stage",
        compiler_params=pltpu.CompilerParams(vmem_limit_bytes=GRANT),
        cost_estimate=pl.CostEstimate(flops=1 << 20, bytes_accessed=2 << 20, transcendentals=0),
    )(*[pltpu.with_memory_space_constraint(x, pltpu.HBM) for x in (vol, adj, mask)])


def coupling_kernel(base, spot_ref, feat_ref, adj_ref, absent_ref, cols_ref, *refs):
    keep_ref, send_ref = refs[-2:]
    rows = feat_ref.shape[0]
    width = cols_ref.shape[2]
    far = (base + pl.program_id(0)) ^ spot_ref[1]

    cols_tiles = absent_ref.shape[1]
    tile = lax.broadcasted_iota(jnp.int32, (cols_tiles, width), 0)
    piece = lax.broadcasted_iota(jnp.int32, (cols_tiles, width), 1) // TILE
    swapped = (piece % 2) * 2 + piece // 2
    pick = jnp.where(tile == 4 * far + (swapped ^ spot_ref[0]), 1.0, 0.0).astype(jnp.bfloat16)
    barred = FAR * jnp.dot(absent_ref[...].astype(jnp.bfloat16), pick, preferred_element_type=jnp.float32)
    target = features(cols_ref[0], True, barred).astype(jnp.bfloat16)

    half = width // 2
    step = 512
    lower = (spot_ref[0] >> 1) & 1
    for side, out_ref in enumerate((keep_ref, send_ref)):
        total = jnp.zeros((adj_ref.shape[0], half), jnp.float32)
        for start in range(0, rows, step):
            d2 = jnp.dot(
                feat_ref[start:start + step, :],
                target[:, side * half:(side + 1) * half],
                preferred_element_type=jnp.float32,
            )
            values = profile(d2).astype(jnp.bfloat16)
            total += jnp.dot(adj_ref[:, start:start + step], values, preferred_element_type=jnp.float32)
        out_ref[lower] = total[:, :TILE]
        out_ref[1 - lower] = total[:, TILE:]


def coupling(base, blocks, spot, staged, cols, earlier=None):
    feat, adj, absent = staged
    count, _, width = cols.shape
    objs = adj.shape[0]
    whole = lambda shape: pl.BlockSpec(shape, lambda i, s: (0,) * len(shape))
    out = jax.ShapeDtypeStruct((2 * blocks, objs, TILE), jnp.float32)
    place = pl.BlockSpec((2, objs, TILE), lambda i, s: ((base + i) ^ s[1], 0, 0))
    extra = () if earlier is None else tuple(earlier)
    return pl.pallas_call(
        functools.partial(coupling_kernel, base),
        grid_spec=pltpu.PrefetchScalarGridSpec(
            num_scalar_prefetch=1,
            grid=(count,),
            in_specs=[
                whole(feat.shape),
                whole(adj.shape),
                whole(absent.shape),
                pl.BlockSpec((1, 8, width), lambda i, s: (i, 0, 0)),
            ] + [pl.BlockSpec(memory_space=pl.ANY)] * len(extra),
            out_specs=[place] * 2,
        ),
        out_shape=(out, out),
        input_output_aliases={5 + i: i for i in range(len(extra))},
        compiler_params=pltpu.CompilerParams(vmem_limit_bytes=GRANT),
        cost_estimate=pl.CostEstimate(flops=20 * feat.shape[0] * count * width, bytes_accessed=2 << 20, transcendentals=0),
    )(spot, feat, adj, absent, cols, *extra)


def gram_kernel(spot_ref, near_ref, far_ref, rows_ref, out_ref, feat_ref):
    @pl.when(pl.program_id(0) == 0)
    def _():
        for j in range(rows_ref.shape[0]):
            feat_ref[:, j * TILE:(j + 1) * TILE] = features(rows_ref[j ^ spot_ref[2]], True).astype(jnp.bfloat16)

    held = near_ref.shape[0]
    block = pl.program_id(0) ^ spot_ref[1]
    slot = lax.rem(block, held)
    points = jnp.where(block < held, near_ref[slot], far_ref[slot])
    lower = (spot_ref[0] >> 1) & 1
    width = out_ref.shape[3]
    step = 256
    for side in range(2):
        one = points[:, 2 * side * TILE:(2 * side + 1) * TILE]
        two = points[:, (2 * side + 1) * TILE:(2 * side + 2) * TILE]
        pair = jnp.where(lower == 0, jnp.concatenate([one, two], axis=1), jnp.concatenate([two, one], axis=1))
        source = features(pair, False).T.astype(jnp.bfloat16)
        for start in range(0, width, step):
            d2 = jnp.dot(source, feat_ref[:, start:start + step], preferred_element_type=jnp.float32)
            out_ref[side, 0, :, start:start + step] = profile(d2).astype(jnp.bfloat16)


def gram(spot, near, far, rows):
    blocks = 2 * near.shape[0]
    width = rows.shape[0] * rows.shape[2]
    whole = lambda shape: pl.BlockSpec(shape, lambda z, s: (0,) * len(shape))
    return pl.pallas_call(
        gram_kernel,
        grid_spec=pltpu.PrefetchScalarGridSpec(
            num_scalar_prefetch=1,
            grid=(blocks,),
            in_specs=[whole(near.shape), whole(far.shape), whole(rows.shape)],
            out_specs=pl.BlockSpec((2, 1, 2 * TILE, width), lambda z, s: (0, z, 0, 0)),
            scratch_shapes=[pltpu.VMEM((DEPTH, width), jnp.bfloat16)],
        ),
        out_shape=pltpu.HBM((2, blocks, 2 * TILE, width), jnp.bfloat16),
        name="gram",
        compiler_params=pltpu.CompilerParams(vmem_limit_bytes=GRANT),
        cost_estimate=pl.CostEstimate(flops=40 * blocks * TILE * width, bytes_accessed=8 << 20, transcendentals=0),
    )(spot, near, far, rows)


def mix_kernel(side, field_ref, gram_ref, *refs):
    out_ref, held_ref, sem_ref = refs[-3:]
    blocks, _, width = held_ref.shape
    objs = field_ref.shape[1]
    copies = [pltpu.make_async_copy(gram_ref.at[side, z], held_ref.at[z], sem_ref.at[z]) for z in range(blocks)]
    for copy in copies:
        copy.start()
    total = jnp.zeros((2 * objs, width), jnp.float32)
    for z in range(blocks):
        field = jnp.concatenate([field_ref[2 * z], field_ref[2 * z + 1]], axis=1)
        high = field.astype(jnp.bfloat16).astype(jnp.float32)
        both = jnp.concatenate([high, field - high], axis=0).astype(jnp.bfloat16)
        copies[z].wait()
        total += jnp.dot(both, held_ref[z], preferred_element_type=jnp.float32)
    for j in range(out_ref.shape[0]):
        part = total[:objs, j * TILE:(j + 1) * TILE] + total[objs:, j * TILE:(j + 1) * TILE]
        out_ref[j] = part if side == 0 else part + refs[0][j]


def mix(side, field, block, earlier=()):
    _, objs, _ = field.shape
    _, blocks, depth, width = block.shape
    parts = width // TILE
    return pl.pallas_call(
        functools.partial(mix_kernel, side),
        in_specs=[pl.BlockSpec(memory_space=pltpu.VMEM), pl.BlockSpec(memory_space=pltpu.HBM)]
        + [pl.BlockSpec(memory_space=pltpu.VMEM)] * len(earlier),
        out_specs=pl.BlockSpec(memory_space=pltpu.VMEM),
        out_shape=jax.ShapeDtypeStruct((parts, objs, TILE), jnp.float32),
        scratch_shapes=[pltpu.VMEM((blocks, depth, width), jnp.bfloat16), pltpu.SemaphoreType.DMA((blocks,))],
        name="mix",
        compiler_params=pltpu.CompilerParams(vmem_limit_bytes=GRANT),
        cost_estimate=pl.CostEstimate(flops=4 * objs * blocks * depth * width, bytes_accessed=5 << 20, transcendentals=0),
    )(field, pltpu.with_memory_space_constraint(block, pltpu.HBM), *earlier)


def body(n_wide, n_narrow, vol_points, vol_adjoint, surf_points, tile_mask):
    half = n_wide // 2
    groups = [[2 * k + core for k in range(half)] for core in range(2)]
    swap = lambda x, bit: lax.ppermute(x, "wide", [(i, i ^ bit) for i in range(n_wide)])
    side = lambda x, bit: lax.ppermute(x, "narrow", [(i, i ^ bit) for i in range(n_narrow)])
    flip = lambda x: swap(x, 1)
    exchange = lambda x: lax.all_to_all(x, "wide", 0, 0, axis_index_groups=groups, tiled=True)
    repeat = lambda x, count: jnp.broadcast_to(x[None], (count,) + x.shape)
    join = lambda x, y: jnp.concatenate([x, y], axis=0)

    wide = lax.axis_index("wide").astype(jnp.int32)
    spot = jnp.stack([wide & 3, wide >> 2, lax.axis_index("narrow").astype(jnp.int32)])
    own = jnp.pad(surf_points, ((0, 5), (0, 0)), constant_values=0.5)
    far = n_wide // 4
    staged = stage(vol_points, vol_adjoint, tile_mask)
    pair = jnp.concatenate([own, swap(own, 2)], axis=1)
    rows = join(own[None], side(own[None], 1))
    quad = jnp.concatenate([pair, flip(pair)], axis=1)[None]
    rows = join(rows, side(rows, 2))
    two = join(quad, swap(quad, 4))
    rows = join(rows, side(rows, 4))
    next_two = swap(two, 8)
    sums = coupling(0, far, spot, staged, two)
    four = join(two, next_two)
    next_four = swap(four, 16)
    sums = coupling(2, far, spot, staged, next_two, sums)
    keep, send = coupling(4, far, spot, staged, next_four, sums)
    got = flip(send)
    block = gram(spot, four, next_four, rows)
    parts = exchange(keep + got)

    total_volume = vol_points.shape[1] * n_wide
    total_surface = surf_points.shape[1] * n_wide * n_narrow
    centre = (LOWER_EDGE + UPPER_EDGE) / 2.0
    half_width = (UPPER_EDGE - LOWER_EDGE) / 2.0
    sigma = centre / half_width
    rho_zero = 1.0 / sigma
    rho_one = 1.0 / (2.0 * sigma - rho_zero)
    gain = KERNEL_GAIN / total_surface * PHI

    def mixed(field):
        mine = exchange(repeat(field, half))
        other = flip(mine)
        partial = mix(0, mine, block)
        partial = mix(1, other, block, (partial,))
        return add_up(lax.all_to_all(partial, "narrow", 0, 0, tiled=True))

    rhs = add_up(parts) * (RHS_GAIN / math.sqrt(total_volume) * PHI)
    first = rhs / centre
    near = rhs - (first + gain * mixed(first))
    update = rho_one * rho_zero * first + 2.0 * rho_one / half_width * near
    solution = first + update
    residual = near - (update + gain * mixed(update))
    return (solution, residual)


def add_up(parts):
    total = parts[0]
    for k in range(1, parts.shape[0]):
        total = total + parts[k]
    return total


def solution(mesh):
    return jax.shard_map(
        functools.partial(body, mesh.shape["wide"], mesh.shape["narrow"]),
        mesh=mesh,
        in_specs=(
            P(None, "wide"),
            P(None, "wide"),
            P(None, ("narrow", "wide")),
            P("wide", "narrow"),
        ),
        out_specs=(P(None, ("narrow", "wide")), P(None, ("narrow", "wide"))),
        check_vma=False,
    )
```

```python
import functools
import math

import jax
import jax.numpy as jnp
from jax import lax
from jax.experimental import pallas as pl
from jax.experimental.pallas import tpu as pltpu
from jax.sharding import PartitionSpec as P


TILE = 128
RADIUS = 0.15
KERNEL_GAIN = 3200.0
RHS_GAIN = 28.0
LOWER_EDGE = 1.0
UPPER_EDGE = 4.0

SCALE = 4.0 / RADIUS
PHI = 1.0 / 256.0
FAR = 4096.0
DEPTH = 128
GRANT = 20 << 20


def split3(x):
    one = x.astype(jnp.bfloat16).astype(jnp.float32)
    rest = x - one
    two = rest.astype(jnp.bfloat16).astype(jnp.float32)
    return one, two, rest - two


def padded(points):
    fill = jnp.full((8 - points.shape[0], points.shape[1]), 0.5, jnp.float32)
    return jnp.concatenate([points, fill], axis=0)


def features(points, target, extra=None):
    count = points.shape[1]
    centred = (points - 0.5) * SCALE
    norm = jnp.sum(centred * centred, axis=0, keepdims=True)
    n1, n2, n3 = split3(jnp.broadcast_to(norm, (8, count)))
    row = lax.broadcasted_iota(jnp.int32, (8, count), 0)
    one, zero = jnp.ones_like(n1), jnp.zeros_like(n1)
    if target:
        c1, c2, c3 = split3(-2.0 * centred)
        tail = jnp.where(row < 3, one, jnp.where(row == 3, n1, jnp.where(row == 4, n2, jnp.where(row == 5, n3, zero))))
        groups = [c1, c2, c1, c2, c3, c1, tail]
    else:
        c1, c2, c3 = split3(centred)
        tail = jnp.where(row == 0, n1, jnp.where(row == 1, n2, jnp.where(row == 2, n3, jnp.where(row < 6, one, zero))))
        groups = [c1, c1, c2, c2, c1, c3, tail]
    used = 8 * len(groups)
    if extra is not None:
        groups.append(extra)
        used += extra.shape[0]
    groups.append(jnp.zeros((DEPTH - used, count), jnp.float32))
    return jnp.concatenate(groups, axis=0)


def profile(d2):
    d2 = jnp.maximum(d2, 1e-12)
    w = jnp.maximum(4.0 - d2 * lax.rsqrt(d2), 0.0)
    square = w * w
    return (square * square) * (5.0 - w)


def stage_kernel(vol_ref, adj_ref, mask_ref, feat_ref, weights_ref, absent_ref, near_ref, held_ref, sem_ref):
    copies = [
        pltpu.make_async_copy(vol_ref, near_ref, sem_ref.at[0]),
        pltpu.make_async_copy(mask_ref, held_ref, sem_ref.at[1]),
        pltpu.make_async_copy(adj_ref, weights_ref, sem_ref.at[2]),
    ]
    for copy in copies:
        copy.start()
    for copy in copies:
        copy.wait()
    rows = vol_ref.shape[1]
    tiles = rows // TILE
    tile = lax.broadcasted_iota(jnp.int32, (tiles, rows), 0)
    place = lax.broadcasted_iota(jnp.int32, (tiles, rows), 1) // TILE
    onehot = jnp.where(tile == place, 1.0, 0.0)
    feat_ref[...] = features(padded(near_ref[...]), False, onehot).T.astype(jnp.bfloat16)
    absent_ref[...] = (1 - held_ref[...]).astype(jnp.float32)


def stage(vol, adj, mask):
    return pl.pallas_call(
        stage_kernel,
        in_specs=[pl.BlockSpec(memory_space=pltpu.HBM)] * 3,
        out_specs=[pl.BlockSpec(memory_space=pltpu.VMEM)] * 3,
        out_shape=(
            jax.ShapeDtypeStruct((vol.shape[1], DEPTH), jnp.bfloat16),
            jax.ShapeDtypeStruct(adj.shape, jnp.bfloat16),
            jax.ShapeDtypeStruct(mask.shape, jnp.float32),
        ),
        scratch_shapes=[
            pltpu.VMEM(vol.shape, jnp.float32),
            pltpu.VMEM(mask.shape, jnp.int32),
            pltpu.SemaphoreType.DMA((3,)),
        ],
        name="stage",
        compiler_params=pltpu.CompilerParams(vmem_limit_bytes=GRANT),
        cost_estimate=pl.CostEstimate(flops=1 << 20, bytes_accessed=2 << 20, transcendentals=0),
    )(*[pltpu.with_memory_space_constraint(x, pltpu.HBM) for x in (vol, adj, mask)])


def coupling_kernel(base, spot_ref, feat_ref, adj_ref, absent_ref, cols_ref, *refs):
    rows = feat_ref.shape[0]
    width = cols_ref.shape[2]
    far = (base + pl.program_id(0)) ^ spot_ref[1]
    lower = (spot_ref[0] >> 1) & 1

    tile = lax.broadcasted_iota(jnp.int32, (absent_ref.shape[1], width), 0)
    piece = lax.broadcasted_iota(jnp.int32, (absent_ref.shape[1], width), 1) // TILE
    swapped = (piece % 2) * 2 + piece // 2
    pick = jnp.where(tile == 4 * far + (swapped ^ spot_ref[0]), 1.0, 0.0).astype(jnp.bfloat16)
    barred = FAR * jnp.dot(absent_ref[...].astype(jnp.bfloat16), pick, preferred_element_type=jnp.float32)
    target = features(cols_ref[0], True, barred).astype(jnp.bfloat16)

    half = width // 2
    step = 512
    for side, out_ref in enumerate(refs[-2:]):
        total = jnp.zeros((adj_ref.shape[0], half), jnp.float32)
        for start in range(0, rows, step):
            d2 = jnp.dot(
                feat_ref[start:start + step, :],
                target[:, side * half:(side + 1) * half],
                preferred_element_type=jnp.float32,
            )
            values = profile(d2).astype(jnp.bfloat16)
            total += jnp.dot(adj_ref[:, start:start + step], values, preferred_element_type=jnp.float32)
        out_ref[lower] = total[:, :TILE]
        out_ref[1 - lower] = total[:, TILE:]


def coupling(base, blocks, spot, staged, cols, earlier=()):
    feat, adj, absent = staged
    count, axes, width = cols.shape
    objs = adj.shape[0]
    whole = lambda shape: pl.BlockSpec(shape, lambda i, s: (0,) * len(shape))
    out = jax.ShapeDtypeStruct((2 * blocks, objs, TILE), jnp.float32)
    place = pl.BlockSpec((2, objs, TILE), lambda i, s: ((base + i) ^ s[1], 0, 0))
    return pl.pallas_call(
        functools.partial(coupling_kernel, base),
        grid_spec=pltpu.PrefetchScalarGridSpec(
            num_scalar_prefetch=1,
            grid=(count,),
            in_specs=[
                whole(feat.shape),
                whole(adj.shape),
                whole(absent.shape),
                pl.BlockSpec((1, axes, width), lambda i, s: (i, 0, 0)),
            ] + [pl.BlockSpec(memory_space=pl.ANY)] * len(earlier),
            out_specs=[place] * 2,
        ),
        out_shape=(out, out),
        input_output_aliases={5 + i: i for i in range(len(earlier))},
        compiler_params=pltpu.CompilerParams(vmem_limit_bytes=GRANT),
        cost_estimate=pl.CostEstimate(
            flops=20 * feat.shape[0] * count * width, bytes_accessed=2 << 20, transcendentals=0
        ),
    )(spot, feat, adj, absent, cols, *earlier)


def gram_kernel(spot_ref, points_ref, rows_ref, out_ref, feat_ref, source_ref):
    lower = (spot_ref[0] >> 1) & 1

    @pl.when((pl.program_id(0) == 0) & (pl.program_id(1) == 0))
    def _():
        slots = [2 * ((j // 2) ^ spot_ref[2]) + ((j % 2) ^ lower) for j in range(rows_ref.shape[0])]
        points = jnp.concatenate([rows_ref[slot] for slot in slots], axis=1)
        whole = features(points, True).astype(jnp.bfloat16)
        part = feat_ref.shape[2]
        for j in range(feat_ref.shape[0]):
            feat_ref[j] = whole[:, j * part:(j + 1) * part]

    @pl.when(pl.program_id(1) == 0)
    def _():
        odd = spot_ref[1] & 1
        pair = (points_ref[odd], points_ref[1 - odd])
        pieces = [part[:, 2 * side * TILE:(2 * side + 1) * TILE] for side in range(2) for part in pair]
        source_ref[...] = features(jnp.concatenate(pieces, axis=1), False).T.astype(jnp.bfloat16)

    source = source_ref[...]
    width = out_ref.shape[3]
    step = 256
    for start in range(0, width, step):
        d2 = jnp.dot(
            source, feat_ref[pl.program_id(1), :, start:start + step], preferred_element_type=jnp.float32
        )
        values = profile(d2).astype(jnp.bfloat16)
        out_ref[0, 0, :, start:start + step] = values[:2 * TILE]
        out_ref[1, 0, :, start:start + step] = values[2 * TILE:]


def gram(spot, points, rows):
    count, axes, lanes = points.shape
    width = rows.shape[0] * rows.shape[2]
    parts = 2
    return pl.pallas_call(
        gram_kernel,
        grid_spec=pltpu.PrefetchScalarGridSpec(
            num_scalar_prefetch=1,
            grid=(count // 2, parts),
            in_specs=[
                pl.BlockSpec((2, axes, lanes), lambda i, k, s: (i, 0, 0)),
                pl.BlockSpec(rows.shape, lambda i, k, s: (0, 0, 0)),
            ],
            out_specs=pl.BlockSpec((2, 1, 2 * TILE, width // parts), lambda i, k, s: (0, i ^ (s[1] >> 1), 0, k)),
            scratch_shapes=[
                pltpu.VMEM((parts, DEPTH, width // parts), jnp.bfloat16),
                pltpu.VMEM((4 * TILE, DEPTH), jnp.bfloat16),
            ],
        ),
        out_shape=pltpu.HBM((2, count // 2, 2 * TILE, width), jnp.bfloat16),
        name="gram",
        compiler_params=pltpu.CompilerParams(vmem_limit_bytes=GRANT),
        cost_estimate=pl.CostEstimate(flops=40 * count * TILE * width, bytes_accessed=8 << 20, transcendentals=0),
    )(spot, points, rows)


def mix_kernel(fresh, side, field_ref, gram_ref, *refs):
    if fresh:
        out_ref, held_ref, sem_ref = refs[-3:]
    else:
        out_ref, held_ref = refs[-1], gram_ref
    blocks, _, width = held_ref.shape
    objs = field_ref.shape[1]
    copies = []
    if fresh:
        copies = [pltpu.make_async_copy(gram_ref.at[side, z], held_ref.at[z], sem_ref.at[z]) for z in range(blocks)]
    for copy in copies:
        copy.start()
    total = jnp.zeros((2 * objs, width), jnp.float32)
    for z in range(blocks):
        field = jnp.concatenate([field_ref[2 * z], field_ref[2 * z + 1]], axis=1)
        high = field.astype(jnp.bfloat16).astype(jnp.float32)
        both = jnp.concatenate([high, field - high], axis=0).astype(jnp.bfloat16)
        if fresh:
            copies[z].wait()
        total += jnp.dot(both, held_ref[z], preferred_element_type=jnp.float32)
    for j in range(out_ref.shape[0]):
        part = total[:objs, j * TILE:(j + 1) * TILE] + total[objs:, j * TILE:(j + 1) * TILE]
        out_ref[j] = part if side == 0 else part + refs[0][j]


def mix(side, field, block, earlier=()):
    fresh = block.ndim == 4
    objs = field.shape[1]
    blocks, depth, width = block.shape[-3:]
    parts = width // TILE
    vmem = pl.BlockSpec(memory_space=pltpu.VMEM)
    out = jax.ShapeDtypeStruct((parts, objs, TILE), jnp.float32)
    place = pltpu.HBM if fresh else pltpu.VMEM
    result = pl.pallas_call(
        functools.partial(mix_kernel, fresh, side),
        in_specs=[vmem, pl.BlockSpec(memory_space=place)] + [vmem] * len(earlier),
        out_specs=[vmem, vmem] if fresh else vmem,
        out_shape=(out, pltpu.VMEM((blocks, depth, width), jnp.bfloat16)) if fresh else out,
        scratch_shapes=[pltpu.SemaphoreType.DMA((blocks,))] if fresh else [],
        name="mix",
        compiler_params=pltpu.CompilerParams(vmem_limit_bytes=GRANT),
        cost_estimate=pl.CostEstimate(flops=4 * objs * blocks * depth * width, bytes_accessed=5 << 20, transcendentals=0),
    )(field, pltpu.with_memory_space_constraint(block, place), *earlier)
    return result if fresh else (result, block)


def body(n_wide, n_narrow, vol_points, vol_adjoint, surf_points, tile_mask):
    far = n_wide // 4
    chips = [[2 * k + core for k in range(2 * far)] for core in range(2)]
    column = [[4 * z + r for z in range(far)] for r in range(4)]
    plane = [
        [n * n_wide + 4 * z + 2 * y + core for n in range(n_narrow) for y in range(2)]
        for z in range(far)
        for core in range(2)
    ]
    swap = lambda x, bit: lax.ppermute(x, "wide", [(i, i ^ bit) for i in range(n_wide)])
    side = lambda x, bit: lax.ppermute(x, "narrow", [(i, i ^ bit) for i in range(n_narrow)])
    repeat = lambda x, count: jnp.broadcast_to(x[None], (count,) + x.shape)
    join = lambda x, y: jnp.concatenate([x, y], axis=0)

    wide = lax.axis_index("wide").astype(jnp.int32)
    spot = jnp.stack([wide & 3, wide >> 2, lax.axis_index("narrow").astype(jnp.int32)])
    own = jnp.pad(surf_points, ((0, 5), (0, 0)), constant_values=0.5)
    staged = stage(vol_points, vol_adjoint, tile_mask)
    across = swap(own, 2)
    pair = jnp.concatenate([own, across], axis=1)
    rows = jnp.stack([own, across])
    quad = jnp.concatenate([pair, swap(pair, 1)], axis=1)[None]
    rows = join(rows, side(rows, 1))
    two = join(quad, swap(quad, 4))
    rows = join(rows, side(rows, 2))
    four = join(two, swap(two, 8))
    rows = join(rows, side(rows, 4))
    next_four = swap(four, 16)
    sums = coupling(0, far, spot, staged, four)
    keep, send = coupling(4, far, spot, staged, next_four, sums)
    got = swap(send, 1)
    block = gram(spot, join(four, next_four), rows)
    parts = lax.all_to_all(keep + got, "wide", 0, 0, axis_index_groups=chips, tiled=True)

    total_volume = vol_points.shape[1] * n_wide
    total_surface = surf_points.shape[1] * n_wide * n_narrow
    centre = (LOWER_EDGE + UPPER_EDGE) / 2.0
    half_width = (UPPER_EDGE - LOWER_EDGE) / 2.0
    sigma = centre / half_width
    rho_zero = 1.0 / sigma
    rho_one = 1.0 / (2.0 * sigma - rho_zero)
    gain = KERNEL_GAIN / total_surface * PHI

    def mixed(field, zero, one):
        mine = lax.all_to_all(repeat(field, far), "wide", 0, 0, axis_index_groups=column, tiled=True)
        other = swap(mine, 1)
        partial, zero = mix(0, mine, zero)
        partial, one = mix(1, other, one, (partial,))
        total = add_up(
            lax.all_to_all(partial, ("narrow", "wide"), 0, 0, axis_index_groups=plane, tiled=True)
        )
        return total, zero, one

    rhs = add_up(parts) * (RHS_GAIN / math.sqrt(total_volume) * PHI)
    first = rhs / centre
    product, zero, one = mixed(first, block, block)
    near = rhs - (first + gain * product)
    update = rho_one * rho_zero * first + 2.0 * rho_one / half_width * near
    solution = first + update
    product, _, _ = mixed(update, zero, one)
    residual = near - (update + gain * product)
    return (solution, residual)


def add_up(parts):
    total = parts[0]
    for k in range(1, parts.shape[0]):
        total = total + parts[k]
    return total


def solution(mesh):
    return jax.shard_map(
        functools.partial(body, mesh.shape["wide"], mesh.shape["narrow"]),
        mesh=mesh,
        in_specs=(
            P(None, "wide"),
            P(None, "wide"),
            P(None, ("narrow", "wide")),
            P("wide", "narrow"),
        ),
        out_specs=(P(None, ("narrow", "wide")), P(None, ("narrow", "wide"))),
        check_vma=False,
    )
```

```python
import functools
import math

import jax
import jax.numpy as jnp
from jax import lax
from jax.experimental import pallas as pl
from jax.experimental.pallas import tpu as pltpu
from jax.sharding import PartitionSpec as P


TILE = 128
RADIUS = 0.15
KERNEL_GAIN = 3200.0
RHS_GAIN = 28.0
LOWER_EDGE = 1.0
UPPER_EDGE = 4.0

SCALE = 4.0 / RADIUS
PHI = 1.0 / 256.0
FAR = 4096.0
DEPTH = 128
GRANT = 20 << 20


def split3(x):
    one = x.astype(jnp.bfloat16).astype(jnp.float32)
    rest = x - one
    two = rest.astype(jnp.bfloat16).astype(jnp.float32)
    return one, two, rest - two


def features(points, target, extra=None):
    count = points.shape[1]
    centred = (points - 0.5) * SCALE
    norm = jnp.sum(centred * centred, axis=0, keepdims=True)
    n1, n2, n3 = split3(jnp.broadcast_to(norm, (8, count)))
    row = lax.broadcasted_iota(jnp.int32, (8, count), 0)
    one, zero = jnp.ones_like(n1), jnp.zeros_like(n1)
    if target:
        c1, c2, c3 = split3(-2.0 * centred)
        tail = jnp.where(row < 3, one, jnp.where(row == 3, n1, jnp.where(row == 4, n2, jnp.where(row == 5, n3, zero))))
        groups = [c1, c2, c1, c2, c3, c1, tail]
    else:
        c1, c2, c3 = split3(centred)
        tail = jnp.where(row == 0, n1, jnp.where(row == 1, n2, jnp.where(row == 2, n3, jnp.where(row < 6, one, zero))))
        groups = [c1, c1, c2, c2, c1, c3, tail]
    used = 8 * len(groups)
    if extra is not None:
        groups.append(extra)
        used += extra.shape[0]
    groups.append(jnp.zeros((DEPTH - used, count), jnp.float32))
    return jnp.concatenate(groups, axis=0)


def profile(d2):
    d2 = jnp.maximum(d2, 1e-12)
    w = jnp.maximum(4.0 - d2 * lax.rsqrt(d2), 0.0)
    square = w * w
    return (square * square) * (5.0 - w)


def stage_kernel(own_ref, other_ref, mask_ref, mask_other_ref, feat_ref, weights_ref, absent_ref):
    rows = own_ref.shape[1]
    objs = weights_ref.shape[0]
    tiles = mask_ref.shape[0]
    for side, (held, held_mask) in enumerate(((own_ref, mask_ref), (other_ref, mask_other_ref))):
        tile = lax.broadcasted_iota(jnp.int32, (2 * tiles, rows), 0)
        place = lax.broadcasted_iota(jnp.int32, (2 * tiles, rows), 1) // TILE + side * tiles
        onehot = jnp.where(tile == place, 1.0, 0.0)
        source = features(held[objs:, :], False, onehot).T.astype(jnp.bfloat16)
        feat_ref[side * rows:(side + 1) * rows, :] = source
        weights_ref[:, side * rows:(side + 1) * rows] = held[:objs, :].astype(jnp.bfloat16)
        absent_ref[side * tiles:(side + 1) * tiles, :] = 1.0 - held_mask[...]


def stage(own, other, mask, mask_other):
    objs = own.shape[0] - 8
    rows = 2 * own.shape[1]
    tiles = 2 * mask.shape[0]
    return pl.pallas_call(
        stage_kernel,
        in_specs=[pl.BlockSpec(memory_space=pltpu.VMEM)] * 4,
        out_specs=[pl.BlockSpec(memory_space=pltpu.VMEM)] * 3,
        out_shape=(
            jax.ShapeDtypeStruct((rows, DEPTH), jnp.bfloat16),
            jax.ShapeDtypeStruct((objs, rows), jnp.bfloat16),
            jax.ShapeDtypeStruct((tiles, mask.shape[1]), jnp.float32),
        ),
        name="stage",
        compiler_params=pltpu.CompilerParams(vmem_limit_bytes=GRANT),
        cost_estimate=pl.CostEstimate(flops=1 << 20, bytes_accessed=2 << 20, transcendentals=0),
    )(own, other, mask, mask_other)


def coupling_kernel(base, spot_ref, feat_ref, adj_ref, absent_ref, cols_ref, *refs):
    out_ref = refs[-1]
    rows = feat_ref.shape[0]
    width = 2 * TILE
    slot = base + 2 * pl.program_id(0)
    lower = (spot_ref[0] >> 1) & 1

    tile = lax.broadcasted_iota(jnp.int32, (absent_ref.shape[1], 2 * width), 0)
    piece = lax.broadcasted_iota(jnp.int32, (absent_ref.shape[1], 2 * width), 1) // TILE
    owner = 4 * ((slot + piece // 2) ^ spot_ref[1]) + ((2 * (piece % 2)) ^ spot_ref[0])
    pick = jnp.where(tile == owner, 1.0, 0.0).astype(jnp.bfloat16)
    barred = FAR * jnp.dot(absent_ref[...].astype(jnp.bfloat16), pick, preferred_element_type=jnp.float32)
    points = jnp.concatenate([cols_ref[k, :, :width] for k in range(2)], axis=1)
    target = features(points, True, barred).astype(jnp.bfloat16)

    step = 512
    for k in range(2):
        total = jnp.zeros((adj_ref.shape[0], width), jnp.float32)
        for start in range(0, rows, step):
            d2 = jnp.dot(
                feat_ref[start:start + step, :],
                target[:, k * width:(k + 1) * width],
                preferred_element_type=jnp.float32,
            )
            values = profile(d2).astype(jnp.bfloat16)
            total += jnp.dot(adj_ref[:, start:start + step], values, preferred_element_type=jnp.float32)
        place = 2 * (k ^ (spot_ref[1] & 1))
        out_ref[place + lower] = total[:, :TILE]
        out_ref[place + 1 - lower] = total[:, TILE:]


def coupling(base, blocks, spot, staged, cols, earlier=()):
    feat, adj, absent = staged
    count, axes, width = cols.shape
    objs = adj.shape[0]
    whole = lambda shape: pl.BlockSpec(shape, lambda i, s: (0,) * len(shape))
    return pl.pallas_call(
        functools.partial(coupling_kernel, base),
        grid_spec=pltpu.PrefetchScalarGridSpec(
            num_scalar_prefetch=1,
            grid=(count // 2,),
            in_specs=[
                whole(feat.shape),
                whole(adj.shape),
                whole(absent.shape),
                pl.BlockSpec((2, axes, width), lambda i, s: (i, 0, 0)),
            ] + [pl.BlockSpec(memory_space=pl.ANY)] * len(earlier),
            out_specs=pl.BlockSpec((4, objs, TILE), lambda i, s: ((base // 2 + i) ^ (s[1] >> 1), 0, 0)),
        ),
        out_shape=jax.ShapeDtypeStruct((2 * blocks, objs, TILE), jnp.float32),
        input_output_aliases={5 + i: i for i in range(len(earlier))},
        compiler_params=pltpu.CompilerParams(vmem_limit_bytes=GRANT),
        cost_estimate=pl.CostEstimate(
            flops=40 * feat.shape[0] * count * TILE, bytes_accessed=2 << 20, transcendentals=0
        ),
    )(spot, feat, adj, absent, cols, *earlier)


def gram_kernel(spot_ref, points_ref, rows_ref, out_ref, feat_ref, source_ref):
    lower = (spot_ref[0] >> 1) & 1

    @pl.when((pl.program_id(0) == 0) & (pl.program_id(1) == 0))
    def _():
        slots = [2 * ((j // 2) ^ spot_ref[2]) + ((j % 2) ^ lower) for j in range(rows_ref.shape[0])]
        points = jnp.concatenate([rows_ref[slot] for slot in slots], axis=1)
        whole = features(points, True).astype(jnp.bfloat16)
        part = feat_ref.shape[2]
        for j in range(feat_ref.shape[0]):
            feat_ref[j] = whole[:, j * part:(j + 1) * part]

    @pl.when(pl.program_id(1) == 0)
    def _():
        odd = spot_ref[1] & 1
        pieces = [points_ref[slot, :, at:at + TILE] for at in (0, 2 * TILE) for slot in (odd, 1 - odd)]
        source_ref[...] = features(jnp.concatenate(pieces, axis=1), False).T.astype(jnp.bfloat16)

    source = source_ref[...]
    width = out_ref.shape[3]
    step = 256
    for start in range(0, width, step):
        d2 = jnp.dot(
            source, feat_ref[pl.program_id(1), :, start:start + step], preferred_element_type=jnp.float32
        )
        values = profile(d2).astype(jnp.bfloat16)
        out_ref[0, 0, :, start:start + step] = values[:2 * TILE]
        out_ref[1, 0, :, start:start + step] = values[2 * TILE:]


def gram(spot, points, rows):
    count, axes, lanes = points.shape
    width = rows.shape[0] * rows.shape[2]
    parts = 2
    return pl.pallas_call(
        gram_kernel,
        grid_spec=pltpu.PrefetchScalarGridSpec(
            num_scalar_prefetch=1,
            grid=(count // 2, parts),
            in_specs=[
                pl.BlockSpec((2, axes, lanes), lambda i, k, s: (i, 0, 0)),
                pl.BlockSpec(rows.shape, lambda i, k, s: (0, 0, 0)),
            ],
            out_specs=pl.BlockSpec((2, 1, 2 * TILE, width // parts), lambda i, k, s: (0, i ^ (s[1] >> 1), 0, k)),
            scratch_shapes=[
                pltpu.VMEM((parts, DEPTH, width // parts), jnp.bfloat16),
                pltpu.VMEM((4 * TILE, DEPTH), jnp.bfloat16),
            ],
        ),
        out_shape=pltpu.HBM((2, count // 2, 2 * TILE, width), jnp.bfloat16),
        name="gram",
        compiler_params=pltpu.CompilerParams(vmem_limit_bytes=GRANT),
        cost_estimate=pl.CostEstimate(flops=40 * count * TILE * width, bytes_accessed=8 << 20, transcendentals=0),
    )(spot, points, rows)


def mix_kernel(fresh, side, field_ref, gram_ref, *refs):
    if fresh:
        out_ref, held_ref, sem_ref = refs[-3:]
    else:
        out_ref, held_ref = refs[-1], gram_ref
    blocks, _, width = held_ref.shape
    objs = field_ref.shape[1]
    copies = []
    if fresh:
        copies = [pltpu.make_async_copy(gram_ref.at[side, z], held_ref.at[z], sem_ref.at[z]) for z in range(blocks)]
    for copy in copies:
        copy.start()
    total = jnp.zeros((2 * objs, width), jnp.float32)
    for z in range(blocks):
        field = jnp.concatenate([field_ref[2 * z], field_ref[2 * z + 1]], axis=1)
        high = field.astype(jnp.bfloat16).astype(jnp.float32)
        both = jnp.concatenate([high, field - high], axis=0).astype(jnp.bfloat16)
        if fresh:
            copies[z].wait()
        total += jnp.dot(both, held_ref[z], preferred_element_type=jnp.float32)
    for j in range(out_ref.shape[0]):
        part = total[:objs, j * TILE:(j + 1) * TILE] + total[objs:, j * TILE:(j + 1) * TILE]
        out_ref[j] = part if side == 0 else part + refs[0][j]


def mix(side, field, block, earlier=()):
    fresh = block.ndim == 4
    objs = field.shape[1]
    blocks, depth, width = block.shape[-3:]
    parts = width // TILE
    vmem = pl.BlockSpec(memory_space=pltpu.VMEM)
    out = jax.ShapeDtypeStruct((parts, objs, TILE), jnp.float32)
    place = pltpu.HBM if fresh else pltpu.VMEM
    result = pl.pallas_call(
        functools.partial(mix_kernel, fresh, side),
        in_specs=[vmem, pl.BlockSpec(memory_space=place)] + [vmem] * len(earlier),
        out_specs=[vmem, vmem] if fresh else vmem,
        out_shape=(out, pltpu.VMEM((blocks, depth, width), jnp.bfloat16)) if fresh else out,
        scratch_shapes=[pltpu.SemaphoreType.DMA((blocks,))] if fresh else [],
        name="mix",
        compiler_params=pltpu.CompilerParams(vmem_limit_bytes=GRANT),
        cost_estimate=pl.CostEstimate(flops=4 * objs * blocks * depth * width, bytes_accessed=5 << 20, transcendentals=0),
    )(field, pltpu.with_memory_space_constraint(block, place), *earlier)
    return result if fresh else (result, block)


def body(n_wide, n_narrow, vol_points, vol_adjoint, surf_points, tile_mask):
    far = n_wide // 4
    chips = [[2 * k + core for k in range(2 * far)] for core in range(2)]
    column = [[4 * z + r for z in range(far)] for r in range(4)]
    plane = [
        [n * n_wide + 4 * z + 2 * y + core for n in range(n_narrow) for y in range(2)]
        for z in range(far)
        for core in range(2)
    ]
    swap = lambda x, bit: lax.ppermute(x, "wide", [(i, i ^ bit) for i in range(n_wide)])
    side = lambda x, bit: lax.ppermute(x, "narrow", [(i, i ^ bit) for i in range(n_narrow)])
    repeat = lambda x, count: jnp.broadcast_to(x[None], (count,) + x.shape)
    join = lambda x, y: jnp.concatenate([x, y], axis=0)

    wide = lax.axis_index("wide").astype(jnp.int32)
    spot = jnp.stack([wide & 3, wide >> 2, lax.axis_index("narrow").astype(jnp.int32)])
    own = jnp.pad(surf_points, ((0, 5), (0, 0)), constant_values=0.5)
    across = swap(own, 2)
    beside = swap(own, 1)
    trio = jnp.concatenate([own, across, beside], axis=1)[None]
    rows = jnp.stack([own, across])
    fill = jnp.full((5, vol_points.shape[1]), 0.5, jnp.float32)
    packed = join(join(vol_adjoint.astype(jnp.float32), vol_points), fill)
    listed = tile_mask.astype(jnp.float32)
    two = join(trio, swap(trio, 4))
    packed_other = swap(packed, 1)
    listed_other = swap(listed, 1)
    four = join(two, swap(two, 8))
    rows = join(rows, side(rows, 1))
    staged = stage(packed, packed_other, listed, listed_other)
    next_four = swap(four, 16)
    rows = join(rows, side(rows, 2))
    sums = coupling(0, far, spot, staged, four)
    rows = join(rows, side(rows, 4))
    sums = coupling(4, far, spot, staged, next_four, (sums,))
    block = gram(spot, join(four, next_four), rows)
    parts = lax.all_to_all(sums, "wide", 0, 0, axis_index_groups=chips, tiled=True)

    total_volume = vol_points.shape[1] * n_wide
    total_surface = surf_points.shape[1] * n_wide * n_narrow
    centre = (LOWER_EDGE + UPPER_EDGE) / 2.0
    half_width = (UPPER_EDGE - LOWER_EDGE) / 2.0
    sigma = centre / half_width
    rho_zero = 1.0 / sigma
    rho_one = 1.0 / (2.0 * sigma - rho_zero)
    gain = KERNEL_GAIN / total_surface * PHI

    def mixed(field, zero, one):
        mine = lax.all_to_all(repeat(field, far), "wide", 0, 0, axis_index_groups=column, tiled=True)
        other = swap(mine, 1)
        partial, zero = mix(0, mine, zero)
        partial, one = mix(1, other, one, (partial,))
        total = add_up(
            lax.all_to_all(partial, ("narrow", "wide"), 0, 0, axis_index_groups=plane, tiled=True)
        )
        return total, zero, one

    rhs = add_up(parts) * (RHS_GAIN / math.sqrt(total_volume) * PHI)
    first = rhs / centre
    product, zero, one = mixed(first, block, block)
    near = rhs - (first + gain * product)
    update = rho_one * rho_zero * first + 2.0 * rho_one / half_width * near
    solution = first + update
    product, _, _ = mixed(update, zero, one)
    residual = near - (update + gain * product)
    return (solution, residual)


def add_up(parts):
    total = parts[0]
    for k in range(1, parts.shape[0]):
        total = total + parts[k]
    return total


def solution(mesh):
    return jax.shard_map(
        functools.partial(body, mesh.shape["wide"], mesh.shape["narrow"]),
        mesh=mesh,
        in_specs=(
            P(None, "wide"),
            P(None, "wide"),
            P(None, ("narrow", "wide")),
            P("wide", "narrow"),
        ),
        out_specs=(P(None, ("narrow", "wide")), P(None, ("narrow", "wide"))),
        check_vma=False,
    )
```

```python
import functools
import math

import jax
import jax.numpy as jnp
from jax import lax
from jax.experimental import pallas as pl
from jax.experimental.pallas import tpu as pltpu
from jax.sharding import PartitionSpec as P


TILE = 128
RADIUS = 0.15
KERNEL_GAIN = 3200.0
RHS_GAIN = 28.0
LOWER_EDGE = 1.0
UPPER_EDGE = 4.0

SCALE = 4.0 / RADIUS
PHI = 1.0 / 256.0
FAR = 4096.0
DEPTH = 128
GRANT = 20 << 20


def split3(x):
    one = x.astype(jnp.bfloat16).astype(jnp.float32)
    rest = x - one
    two = rest.astype(jnp.bfloat16).astype(jnp.float32)
    return one, two, rest - two


def features(points, target, extra=None):
    count = points.shape[1]
    centred = (points - 0.5) * SCALE
    norm = jnp.sum(centred * centred, axis=0, keepdims=True)
    n1, n2, n3 = split3(jnp.broadcast_to(norm, (8, count)))
    row = lax.broadcasted_iota(jnp.int32, (8, count), 0)
    one, zero = jnp.ones_like(n1), jnp.zeros_like(n1)
    if target:
        c1, c2, c3 = split3(-2.0 * centred)
        tail = jnp.where(row < 3, one, jnp.where(row == 3, n1, jnp.where(row == 4, n2, jnp.where(row == 5, n3, zero))))
        groups = [c1, c2, c1, c2, c3, c1, tail]
    else:
        c1, c2, c3 = split3(centred)
        tail = jnp.where(row == 0, n1, jnp.where(row == 1, n2, jnp.where(row == 2, n3, jnp.where(row < 6, one, zero))))
        groups = [c1, c1, c2, c2, c1, c3, tail]
    used = 8 * len(groups)
    if extra is not None:
        groups.append(extra)
        used += extra.shape[0]
    groups.append(jnp.zeros((DEPTH - used, count), jnp.float32))
    return jnp.concatenate(groups, axis=0)


def profile(d2):
    d2 = jnp.maximum(d2, 1e-12)
    w = jnp.maximum(4.0 - d2 * lax.rsqrt(d2), 0.0)
    square = w * w
    return (square * square) * (5.0 - w)


def stage_kernel(own_ref, other_ref, mask_ref, mask_other_ref, feat_ref, weights_ref, absent_ref):
    rows = own_ref.shape[1]
    objs = weights_ref.shape[0]
    tiles = mask_ref.shape[0]
    for side, (held, held_mask) in enumerate(((own_ref, mask_ref), (other_ref, mask_other_ref))):
        tile = lax.broadcasted_iota(jnp.int32, (2 * tiles, rows), 0)
        place = lax.broadcasted_iota(jnp.int32, (2 * tiles, rows), 1) // TILE + side * tiles
        onehot = jnp.where(tile == place, 1.0, 0.0)
        source = features(held[objs:, :], False, onehot).T.astype(jnp.bfloat16)
        feat_ref[side * rows:(side + 1) * rows, :] = source
        weights_ref[:, side * rows:(side + 1) * rows] = held[:objs, :].astype(jnp.bfloat16)
        absent_ref[side * tiles:(side + 1) * tiles, :] = 1.0 - held_mask[...]


def stage(own, other, mask, mask_other):
    objs = own.shape[0] - 8
    rows = 2 * own.shape[1]
    tiles = 2 * mask.shape[0]
    return pl.pallas_call(
        stage_kernel,
        in_specs=[pl.BlockSpec(memory_space=pltpu.VMEM)] * 4,
        out_specs=[pl.BlockSpec(memory_space=pltpu.VMEM)] * 3,
        out_shape=(
            jax.ShapeDtypeStruct((rows, DEPTH), jnp.bfloat16),
            jax.ShapeDtypeStruct((objs, rows), jnp.bfloat16),
            jax.ShapeDtypeStruct((tiles, mask.shape[1]), jnp.float32),
        ),
        name="stage",
        compiler_params=pltpu.CompilerParams(vmem_limit_bytes=GRANT),
        cost_estimate=pl.CostEstimate(flops=1 << 20, bytes_accessed=2 << 20, transcendentals=0),
    )(own, other, mask, mask_other)


def coupling_kernel(base, spot_ref, feat_ref, adj_ref, absent_ref, cols_ref, *refs):
    out_ref = refs[-1]
    rows = feat_ref.shape[0]
    width = 2 * TILE
    group = cols_ref.shape[0]
    slot = base + group * pl.program_id(0)
    lower = (spot_ref[0] >> 1) & 1

    tile = lax.broadcasted_iota(jnp.int32, (absent_ref.shape[1], group * width), 0)
    piece = lax.broadcasted_iota(jnp.int32, (absent_ref.shape[1], group * width), 1) // TILE
    owner = 4 * ((slot + piece // 2) ^ spot_ref[1]) + ((2 * (piece % 2)) ^ spot_ref[0])
    pick = jnp.where(tile == owner, 1.0, 0.0).astype(jnp.bfloat16)
    barred = FAR * jnp.dot(absent_ref[...].astype(jnp.bfloat16), pick, preferred_element_type=jnp.float32)
    points = jnp.concatenate([cols_ref[k, :, :width] for k in range(group)], axis=1)
    target = features(points, True, barred).astype(jnp.bfloat16)

    step = 512
    for k in range(group):
        total = jnp.zeros((adj_ref.shape[0], width), jnp.float32)
        for start in range(0, rows, step):
            d2 = jnp.dot(
                feat_ref[start:start + step, :],
                target[:, k * width:(k + 1) * width],
                preferred_element_type=jnp.float32,
            )
            values = profile(d2).astype(jnp.bfloat16)
            total += jnp.dot(adj_ref[:, start:start + step], values, preferred_element_type=jnp.float32)
        place = 2 * (k ^ (spot_ref[1] & (group - 1)))
        out_ref[place + lower] = total[:, :TILE]
        out_ref[place + 1 - lower] = total[:, TILE:]


def coupling(base, blocks, spot, staged, cols, earlier=()):
    feat, adj, absent = staged
    count, axes, width = cols.shape
    objs = adj.shape[0]
    group = 4
    whole = lambda shape: pl.BlockSpec(shape, lambda i, s: (0,) * len(shape))
    return pl.pallas_call(
        functools.partial(coupling_kernel, base),
        grid_spec=pltpu.PrefetchScalarGridSpec(
            num_scalar_prefetch=1,
            grid=(count // group,),
            in_specs=[
                whole(feat.shape),
                whole(adj.shape),
                whole(absent.shape),
                pl.BlockSpec((group, axes, width), lambda i, s: (i, 0, 0)),
            ] + [pl.BlockSpec(memory_space=pl.ANY)] * len(earlier),
            out_specs=pl.BlockSpec((2 * group, objs, TILE), lambda i, s: ((base // group + i) ^ (s[1] // group), 0, 0)),
        ),
        out_shape=jax.ShapeDtypeStruct((2 * blocks, objs, TILE), jnp.float32),
        input_output_aliases={5 + i: i for i in range(len(earlier))},
        compiler_params=pltpu.CompilerParams(vmem_limit_bytes=GRANT),
        cost_estimate=pl.CostEstimate(
            flops=40 * feat.shape[0] * count * TILE, bytes_accessed=2 << 20, transcendentals=0
        ),
    )(spot, feat, adj, absent, cols, *earlier)


def gram_kernel(spot_ref, points_ref, rows_ref, out_ref, feat_ref, source_ref):
    lower = (spot_ref[0] >> 1) & 1

    @pl.when((pl.program_id(0) == 0) & (pl.program_id(1) == 0))
    def _():
        slots = [2 * ((j // 2) ^ spot_ref[2]) + ((j % 2) ^ lower) for j in range(rows_ref.shape[0])]
        points = jnp.concatenate([rows_ref[slot] for slot in slots], axis=1)
        whole = features(points, True).astype(jnp.bfloat16)
        part = feat_ref.shape[2]
        for j in range(feat_ref.shape[0]):
            feat_ref[j] = whole[:, j * part:(j + 1) * part]

    @pl.when(pl.program_id(1) == 0)
    def _():
        odd = spot_ref[1] & 1
        pieces = [points_ref[slot, :, at:at + TILE] for at in (0, 2 * TILE) for slot in (odd, 1 - odd)]
        source_ref[...] = features(jnp.concatenate(pieces, axis=1), False).T.astype(jnp.bfloat16)

    source = source_ref[...]
    width = out_ref.shape[3]
    step = 256
    for start in range(0, width, step):
        d2 = jnp.dot(
            source, feat_ref[pl.program_id(1), :, start:start + step], preferred_element_type=jnp.float32
        )
        values = profile(d2).astype(jnp.bfloat16)
        out_ref[0, 0, :, start:start + step] = values[:2 * TILE]
        out_ref[1, 0, :, start:start + step] = values[2 * TILE:]


def gram(spot, points, rows):
    count, axes, lanes = points.shape
    width = rows.shape[0] * rows.shape[2]
    parts = 2
    return pl.pallas_call(
        gram_kernel,
        grid_spec=pltpu.PrefetchScalarGridSpec(
            num_scalar_prefetch=1,
            grid=(count // 2, parts),
            in_specs=[
                pl.BlockSpec((2, axes, lanes), lambda i, k, s: (i, 0, 0)),
                pl.BlockSpec(rows.shape, lambda i, k, s: (0, 0, 0)),
            ],
            out_specs=pl.BlockSpec((2, 1, 2 * TILE, width // parts), lambda i, k, s: (0, i ^ (s[1] >> 1), 0, k)),
            scratch_shapes=[
                pltpu.VMEM((parts, DEPTH, width // parts), jnp.bfloat16),
                pltpu.VMEM((4 * TILE, DEPTH), jnp.bfloat16),
            ],
        ),
        out_shape=pltpu.HBM((2, count // 2, 2 * TILE, width), jnp.bfloat16),
        name="gram",
        compiler_params=pltpu.CompilerParams(vmem_limit_bytes=GRANT),
        cost_estimate=pl.CostEstimate(flops=40 * count * TILE * width, bytes_accessed=8 << 20, transcendentals=0),
    )(spot, points, rows)


def mix_kernel(fresh, side, field_ref, gram_ref, *refs):
    if fresh:
        out_ref, held_ref, sem_ref = refs[-3:]
    else:
        out_ref, held_ref = refs[-1], gram_ref
    blocks, _, width = held_ref.shape
    objs = field_ref.shape[1]
    copies = []
    if fresh:
        copies = [pltpu.make_async_copy(gram_ref.at[side, z], held_ref.at[z], sem_ref.at[z]) for z in range(blocks)]
    for copy in copies:
        copy.start()
    total = jnp.zeros((2 * objs, width), jnp.float32)
    for z in range(blocks):
        field = jnp.concatenate([field_ref[2 * z], field_ref[2 * z + 1]], axis=1)
        high = field.astype(jnp.bfloat16).astype(jnp.float32)
        both = jnp.concatenate([high, field - high], axis=0).astype(jnp.bfloat16)
        if fresh:
            copies[z].wait()
        total += jnp.dot(both, held_ref[z], preferred_element_type=jnp.float32)
    for j in range(out_ref.shape[0]):
        part = total[:objs, j * TILE:(j + 1) * TILE] + total[objs:, j * TILE:(j + 1) * TILE]
        out_ref[j] = part if side == 0 else part + refs[0][j]


def mix(side, field, block, earlier=()):
    fresh = block.ndim == 4
    objs = field.shape[1]
    blocks, depth, width = block.shape[-3:]
    parts = width // TILE
    vmem = pl.BlockSpec(memory_space=pltpu.VMEM)
    out = jax.ShapeDtypeStruct((parts, objs, TILE), jnp.float32)
    place = pltpu.HBM if fresh else pltpu.VMEM
    result = pl.pallas_call(
        functools.partial(mix_kernel, fresh, side),
        in_specs=[vmem, pl.BlockSpec(memory_space=place)] + [vmem] * len(earlier),
        out_specs=[vmem, vmem] if fresh else vmem,
        out_shape=(out, pltpu.VMEM((blocks, depth, width), jnp.bfloat16)) if fresh else out,
        scratch_shapes=[pltpu.SemaphoreType.DMA((blocks,))] if fresh else [],
        name="mix",
        compiler_params=pltpu.CompilerParams(vmem_limit_bytes=GRANT),
        cost_estimate=pl.CostEstimate(flops=4 * objs * blocks * depth * width, bytes_accessed=5 << 20, transcendentals=0),
    )(field, pltpu.with_memory_space_constraint(block, place), *earlier)
    return result if fresh else (result, block)


def body(n_wide, n_narrow, vol_points, vol_adjoint, surf_points, tile_mask):
    far = n_wide // 4
    chips = [[2 * k + core for k in range(2 * far)] for core in range(2)]
    column = [[4 * z + r for z in range(far)] for r in range(4)]
    plane = [
        [n * n_wide + 4 * z + 2 * y + core for n in range(n_narrow) for y in range(2)]
        for z in range(far)
        for core in range(2)
    ]
    swap = lambda x, bit: lax.ppermute(x, "wide", [(i, i ^ bit) for i in range(n_wide)])
    side = lambda x, bit: lax.ppermute(x, "narrow", [(i, i ^ bit) for i in range(n_narrow)])
    repeat = lambda x, count: jnp.broadcast_to(x[None], (count,) + x.shape)
    join = lambda x, y: jnp.concatenate([x, y], axis=0)

    wide = lax.axis_index("wide").astype(jnp.int32)
    spot = jnp.stack([wide & 3, wide >> 2, lax.axis_index("narrow").astype(jnp.int32)])
    own = jnp.pad(surf_points, ((0, 5), (0, 0)), constant_values=0.5)
    across = swap(own, 2)
    beside = swap(own, 1)
    trio = jnp.concatenate([own, across, beside], axis=1)[None]
    rows = jnp.stack([own, across])
    fill = jnp.full((5, vol_points.shape[1]), 0.5, jnp.float32)
    packed = join(join(vol_adjoint.astype(jnp.float32), vol_points), fill)
    listed = tile_mask.astype(jnp.float32)
    two = join(trio, swap(trio, 4))
    packed_other = swap(packed, 1)
    listed_other = swap(listed, 1)
    four = join(two, swap(two, 8))
    rows = join(rows, side(rows, 1))
    staged = stage(packed, packed_other, listed, listed_other)
    next_four = swap(four, 16)
    rows = join(rows, side(rows, 2))
    sums = coupling(0, far, spot, staged, four)
    rows = join(rows, side(rows, 4))
    sums = coupling(4, far, spot, staged, next_four, (sums,))
    block = gram(spot, join(four, next_four), rows)
    parts = lax.all_to_all(sums, "wide", 0, 0, axis_index_groups=chips, tiled=True)

    total_volume = vol_points.shape[1] * n_wide
    total_surface = surf_points.shape[1] * n_wide * n_narrow
    centre = (LOWER_EDGE + UPPER_EDGE) / 2.0
    half_width = (UPPER_EDGE - LOWER_EDGE) / 2.0
    sigma = centre / half_width
    rho_zero = 1.0 / sigma
    rho_one = 1.0 / (2.0 * sigma - rho_zero)
    gain = KERNEL_GAIN / total_surface * PHI

    def mixed(field, zero, one):
        mine = lax.all_to_all(repeat(field, far), "wide", 0, 0, axis_index_groups=column, tiled=True)
        other = swap(mine, 1)
        partial, zero = mix(0, mine, zero)
        partial, one = mix(1, other, one, (partial,))
        total = add_up(
            lax.all_to_all(partial, ("narrow", "wide"), 0, 0, axis_index_groups=plane, tiled=True)
        )
        return total, zero, one

    rhs = add_up(parts) * (RHS_GAIN / math.sqrt(total_volume) * PHI)
    first = rhs / centre
    product, zero, one = mixed(first, block, block)
    near = rhs - (first + gain * product)
    update = rho_one * rho_zero * first + 2.0 * rho_one / half_width * near
    solution = first + update
    product, _, _ = mixed(update, zero, one)
    residual = near - (update + gain * product)
    return (solution, residual)


def add_up(parts):
    total = parts[0]
    for k in range(1, parts.shape[0]):
        total = total + parts[k]
    return total


def solution(mesh):
    return jax.shard_map(
        functools.partial(body, mesh.shape["wide"], mesh.shape["narrow"]),
        mesh=mesh,
        in_specs=(
            P(None, "wide"),
            P(None, "wide"),
            P(None, ("narrow", "wide")),
            P("wide", "narrow"),
        ),
        out_specs=(P(None, ("narrow", "wide")), P(None, ("narrow", "wide"))),
        check_vma=False,
    )
```
